32 devices in a mesh: dp: 16 (over z, x, core), fsdp: 2 (over y).
Axes of the slice: x: 2, y: 2, z: 4, core: 2. Of those that a mesh axis runs over, the one named last changes fastest.
Arguments:
- inputs: bfloat16 [128, 256, 512], P(('dp', 'fsdp')), may hold values from -0.3125 to 0.3125
- out_grad: bfloat16 [128, 256, 512], P(('dp', 'fsdp')), may hold values from -6 to 6
- coeff_fixed: int32 [128, 16], P(('dp', 'fsdp')), may hold values from 0 to 4096
- atom_counts: int32 [128], P(('dp', 'fsdp')), may hold values from 64 to 256, as said below
- experts: bfloat16 [16, 512, 512], P(None, ('dp', 'fsdp')), may hold values from -0.125 to 0.125
Outputs:
- in_grad: bfloat16 [128, 256, 512], P(('dp', 'fsdp'))
- expert_grad: float32 [16, 512, 512], P(None, ('dp', 'fsdp'))
The draws below stay inside these ranges and needn't reach their ends.
Inputs may be any that keep to these rules, and one draw needn't show every extreme that they name: `atom_counts`: some system has exactly 256 atoms and some exactly 64.
All inputs are finite; a program needn't handle non-finite values.
Results may differ from the reference program's by a relative error of at most 0.0049.
Values may be sent and summed in bfloat16 or wider, within the bound.
A program may use at most 128 MiB of HBM per device.

```python
import jax
import jax.numpy as jnp
from jax import lax

D = 512
EXPERTS = 16
SYS_DEV = 4
MAX_ATOMS = 256
SYSTEMS = 128


def draw_atom_counts(key, part):
    first = jax.random.fold_in(key, 11)
    second = jax.random.fold_in(key, 12)
    counts = jax.random.randint(first, (SYSTEMS,), MAX_ATOMS // 4, MAX_ATOMS + 1, dtype=jnp.int32)
    where = jax.random.randint(second, (), 0, SYSTEMS, dtype=jnp.int32)
    counts = counts.at[where].set(MAX_ATOMS)
    counts = counts.at[(where + 1) % SYSTEMS].set(MAX_ATOMS // 4)
    return counts


def touch_ends(array, rng, smallest, largest):
    dims = array.shape
    place = [jax.random.randint(jax.random.fold_in(rng, axis), (), 0, dims[axis]) for axis in range(len(dims))]
    array = array.at[tuple(place)].set(smallest)
    longest = dims.index(max(dims))
    place[longest] = (place[longest] + 1) % dims[longest]
    return array.at[tuple(place)].set(largest)


def spiked(result, own_key, source, target, blocks, factor):
    owner, partner = [(jnp.arange(result.shape[dim]) // (result.shape[dim] // blocks)).reshape([-1 if axis == dim else 1 for axis in range(result.ndim)]) for dim in (source, target)]
    chosen = jax.random.permutation(own_key, blocks)[partner]
    strong = (owner == chosen) | (owner == (partner + blocks // 2) % blocks)
    return jnp.where(strong, factor * result, result)


def shard_levels(rng, dims, cuts, low, top_value):
    gain, own = 1.0, jax.random.fold_in(rng, 6)
    for position, shards_of in cuts:
        draws = jnp.exp(jax.random.uniform(jax.random.fold_in(own, position), (shards_of,), jnp.float32, low / len(cuts), top_value / len(cuts)))
        gain = gain * jnp.repeat(draws, dims[position] // shards_of).reshape([-1 if axis == position else 1 for axis in range(len(dims))])
    return gain


def noise(stream_key, shape, deviation, most, split=(), kind=jnp.bfloat16):
    array = deviation * jax.random.normal(stream_key, shape, jnp.float32)
    if split:
        array = array * shard_levels(stream_key, shape, split, -0.22, 0.18)
    return jnp.clip(array, -most, most).astype(kind)


def heavy_noise(own_key, dims, scale, reach, split, heavy, held_as=jnp.bfloat16):
    entries = scale * jax.random.normal(own_key, dims, jnp.float32)
    if split:
        entries = entries * shard_levels(own_key, dims, split, -0.22, 0.18)
    return jnp.clip(spiked(entries, jax.random.fold_in(own_key, 3), *heavy), -reach, reach).astype(held_as)


def setup_inputs(seed: int = 0) -> dict:
    streams_of = jax.random.split(jax.random.key(seed), 6)
    inputs = heavy_noise(streams_of[0], (SYSTEMS, MAX_ATOMS, D), (2.0 / (SYSTEMS * MAX_ATOMS) ** 0.5), 0.3125, ((0, 32),), (0, 2, 32, 2.75))
    out_grad = noise(streams_of[1], (SYSTEMS, MAX_ATOMS, D), 1.0, 6.0, ((0, 32),))
    coeff_fixed = touch_ends(jax.random.randint(streams_of[2], (SYSTEMS, EXPERTS), 0, 4097), jax.random.fold_in(streams_of[2], 1), 0, 4096).astype(jnp.int32)
    atom_counts = draw_atom_counts(jax.random.fold_in(streams_of[5], 71), 0)
    experts = noise(streams_of[4], (EXPERTS, D, D), (4 * D) ** -0.5, 0.125, ((1, 32),))
    return dict(inputs=inputs, out_grad=out_grad, coeff_fixed=coeff_fixed, atom_counts=atom_counts, experts=experts)


HIGH = lax.Precision.HIGHEST


def reference(inputs, out_grad, coeff_fixed, atom_counts, experts):
    nsys = inputs.shape[0]
    blocks = nsys // SYS_DEV
    flat_experts = experts.astype(jnp.float32).reshape(EXPERTS, D * D)
    xs = inputs.reshape(blocks, SYS_DEV, MAX_ATOMS, D)
    gs = out_grad.reshape(blocks, SYS_DEV, MAX_ATOMS, D)
    qs = coeff_fixed.reshape(blocks, SYS_DEV, EXPERTS)
    ns = atom_counts.reshape(blocks, SYS_DEV)

    def step(total, block):
        acts, grads, fixed, counts = block
        coeffs = fixed.astype(jnp.float32) / 4096.0
        valid = jnp.arange(MAX_ATOMS, dtype=jnp.int32)[None, :] < counts[:, None]
        masked = jnp.where(valid[:, :, None], grads, jnp.zeros_like(grads)).astype(jnp.float32)
        merged = jnp.dot(coeffs, flat_experts, precision=HIGH).reshape(SYS_DEV, D, D)
        merged = lax.optimization_barrier(merged.astype(jnp.bfloat16)).astype(jnp.float32)
        in_grad = jnp.einsum("smj,sij->smi", masked, merged, precision=HIGH).astype(jnp.bfloat16)
        per_system = jnp.einsum("smi,smj->sij", acts.astype(jnp.float32), masked, precision=HIGH)
        total = total + jnp.einsum("se,sij->eij", coeffs, per_system, precision=HIGH)
        return total, in_grad

    total, in_grads = lax.scan(step, jnp.zeros((EXPERTS, D, D), jnp.float32), (xs, gs, qs, ns))
    return in_grads.reshape(nsys, MAX_ATOMS, D), total
```

```python
import functools

import jax
import jax.numpy as jnp
from jax import lax
from jax.experimental import pallas as pl
from jax.experimental.pallas import tpu as pltpu
from jax.sharding import PartitionSpec as P

HIGH = lax.Precision.HIGHEST
MESH = pl.DeviceIdType.MESH
BF16 = jnp.bfloat16
F32 = jnp.float32


def dot(a, b, ca, cb):
    return lax.dot_general(a, b, (((ca,), (cb,)), ((), ())), preferred_element_type=F32)


def kernel(nz, n_sys, n_exp, rows, width,
           counts_ref, in_ref, og_ref, ex_ref, kl_ref,
           ig_ref, eg_ref,
           mk, pb, g, eo, eb, er, zs, zr, xg, ka, kr, mb, mr,
           loc, ka_s, ka_r, kr_s, kr_r, xz_s, xz_r, xy_s, xy_r,
           pb_s, pb_r, eb_s, eb_r, zs_s, zs_r, mb_s, mb_r):
    dp = lax.axis_index("dp")
    y = lax.axis_index("fsdp")
    z = dp // 4
    x = lax.rem(dp // 2, 2)
    c = lax.rem(dp, 2)
    sr = n_sys * rows
    er_rows = n_exp * rows

    def flip(v, d):
        return lax.rem(v + d, 2)

    def at(zz, xx, cc, yy):
        return ((zz * 2 + xx) * 2 + cc, yy)

    def zto(k):
        return lax.rem(z + k, nz)

    def zfrom(k):
        return lax.rem(z + nz - k, nz)

    rest = (1, 2, 3)
    peers = [at(z, x, flip(c, 1), y)]
    peers += [at(z, flip(x, 1), flip(c, d), y) for d in (0, 1)]
    peers += [at(z, x, flip(c, d), flip(y, 1)) for d in (0, 1)]
    peers += [at(zto(k), x, c, y) for k in range(1, nz)]
    barrier = pltpu.get_barrier_semaphore()
    for peer in peers:
        pl.semaphore_signal(barrier, inc=1, device_id=peer, device_id_type=MESH)
    pl.semaphore_wait(barrier, len(peers))

    def send(src, dst, s, r, peer):
        copy = pltpu.make_async_remote_copy(
            src_ref=src, dst_ref=dst, send_sem=s, recv_sem=r, device_id=peer, device_id_type=MESH
        )
        copy.start()
        return copy

    n_loc = [0]

    def local(src, dst):
        copy = pltpu.make_async_copy(src, dst, loc.at[n_loc[0]])
        n_loc[0] += 1
        copy.start()
        return copy

    sent = []
    xc = x * 2 + c
    yc = y * 2 + c

    ka_c, kr_c, xz_c, xy_c = [], [], [], []
    for j in rest:
        ka_c.append(send(kl_ref, ka.at[xc], ka_s.at[j - 1], ka_r.at[j - 1],
                         at(z, flip(x, j // 2), flip(c, j % 2), y)))
        kr_c.append(send(kl_ref, kr.at[yc], kr_s.at[j - 1], kr_r.at[j - 1],
                         at(z, x, flip(c, j % 2), flip(y, j // 2))))
    ka_own = local(kl_ref, ka.at[xc])
    kr_own = local(kl_ref, kr.at[yc])
    for k in range(1, nz):
        xz_c.append(send(ex_ref, xg.at[y, z], xz_s.at[k], xz_r.at[k], at(zto(k), x, c, y)))
    xy_c.append(send(ex_ref, xg.at[y, z], xy_s.at[0], xy_r.at[0], at(z, x, c, flip(y, 1))))
    ex_own = local(ex_ref, xg.at[y, z])
    sent += ka_c + kr_c + xz_c + xy_c

    for s in range(n_sys):
        slot = lax.broadcasted_iota(jnp.int32, og_ref.shape[1:], 0)
        mk[s] = jnp.where(slot < counts_ref[s], og_ref[s], jnp.zeros(og_ref.shape[1:], BF16))
        prod = dot(in_ref[s], mk[s], 0, 0).astype(BF16)
        for b in range(width // rows):
            yy, cc, xx, zz = b % 2, b // 2 % 2, b // 4 % 2, b // 8
            pb[yy * 2 + cc, zz, xx, s * rows:(s + 1) * rows, :] = prod[b * rows:(b + 1) * rows, :]
    order = list(range(1, nz)) + [0]
    pb_c, g_own = {}, {}
    for k in order:
        for j in rest:
            yy, cc = flip(y, j // 2), flip(c, j % 2)
            pb_c[k, j] = send(pb.at[yy * 2 + cc, zto(k)], g.at[k, :, yc],
                              pb_s.at[k, j - 1], pb_r.at[k, j - 1], at(z, x, cc, yy))
        g_own[k] = local(pb.at[yc, zto(k)], g.at[k, :, yc])
    sent += list(pb_c.values())

    mb_c, m_own = {}, {}

    def merge(ky, k):
        yy = flip(y, ky)
        zz = zfrom(k)
        block = xg[yy, zz]
        high = ka[:, 0].reshape(4 * sr, er_rows)
        low = ka[:, 1].reshape(4 * sr, er_rows)
        mb[ky, k] = (dot(high, block, 1, 0) + dot(low, block, 1, 0)).astype(BF16).reshape(
            4, n_sys, rows, width)
        for j in rest:
            xx, cc = flip(x, j // 2), flip(c, j % 2)
            mb_c[ky, k, j] = send(mb.at[ky, k, xx * 2 + cc], mr.at[:, zz, xc, yy],
                                  mb_s.at[ky, k, j - 1], mb_r.at[ky, k, j - 1], at(z, xx, cc, y))
            sent.append(mb_c[ky, k, j])
        m_own[ky, k] = local(mb.at[ky, k, xc], mr.at[:, zz, xc, yy])

    def expert_term(k, xx):
        block = g[k, xx].reshape(4 * sr, width)
        high = kr[:, 0].reshape(4 * sr, er_rows)
        low = kr[:, 1].reshape(4 * sr, er_rows)
        return dot(high, block, 0, 0) + dot(low, block, 0, 0)

    ka_own.wait()
    kr_own.wait()
    ex_own.wait()
    for copy in ka_c + kr_c:
        copy.wait_recv()
    merge(0, 0)
    eb_c = {}
    for k in order:
        if k:
            xz_c[k - 1].wait_recv()
            xy_c.append(send(xg.at[y, zfrom(k)], xg.at[y, zfrom(k)], xy_s.at[k], xy_r.at[k],
                             at(z, x, c, flip(y, 1))))
            sent.append(xy_c[-1])
            merge(0, k)
        g_own[k].wait()
        for j in rest:
            pb_c[k, j].wait_recv()
        eb[k] = expert_term(k, flip(x, 1)).astype(BF16)
        eb_c[k] = send(eb.at[k], er.at[k], eb_s.at[k], eb_r.at[k], at(z, flip(x, 1), c, y))
        sent.append(eb_c[k])
        eo[k] = expert_term(k, x)
    zs_c = {}
    for n, k in enumerate(order):
        eb_c[k].wait_recv()
        total = eo[k] + er[k].astype(F32)
        if k:
            zs[k] = total.astype(BF16)
            zs_c[k] = send(zs.at[k], zr.at[k], zs_s.at[k], zs_r.at[k], at(zto(k), x, c, y))
            sent.append(zs_c[k])
        else:
            eo[0] = total
        xy_c[n].wait_recv()
        merge(1, n)
    for key in mb_c:
        mb_c[key].wait_recv()
    for key in m_own:
        m_own[key].wait()
    for s in range(n_sys):
        ig_ref[s] = dot(mk[s], mr[s].reshape(width, width), 1, 1).astype(BF16)
    total = eo[0]
    for k in range(1, nz):
        zs_c[k].wait_recv()
        total = total + zr[k].astype(F32)
    eg_ref[...] = total
    for copy in sent:
        copy.wait_send()


def fused(inputs, out_grad, coeff_fixed, atom_counts, experts, nz):
    n_sys, n_slots, width = inputs.shape
    n_exp, rows, _ = experts.shape
    sr, er_rows = n_sys * rows, n_exp * rows
    high = (coeff_fixed // 64).astype(F32) / 64.0
    low = (coeff_fixed % 64).astype(F32) / 4096.0
    halves = jnp.stack([high, low])
    eye = jnp.eye(rows, dtype=F32)
    kl = (halves[:, :, None, :, None] * eye[None, None, :, None, :]).reshape(2, sr, er_rows).astype(BF16)
    vmem = pl.BlockSpec(memory_space=pltpu.VMEM)
    dma = pltpu.SemaphoreType.DMA
    in_grad, expert_grad = pl.pallas_call(
        functools.partial(kernel, nz, n_sys, n_exp, rows, width),
        out_shape=(
            jax.ShapeDtypeStruct(inputs.shape, BF16),
            jax.ShapeDtypeStruct((er_rows, width), F32),
        ),
        in_specs=[pl.BlockSpec(memory_space=pltpu.SMEM)] + [vmem] * 4,
        out_specs=(vmem, vmem),
        scratch_shapes=[
            pltpu.VMEM(out_grad.shape, BF16),
            pltpu.VMEM((4, nz, 2, sr, width), BF16),
            pltpu.VMEM((nz, 2, 4, sr, width), BF16),
            pltpu.VMEM((nz, er_rows, width), F32),
            pltpu.VMEM((nz, er_rows, width), BF16),
            pltpu.VMEM((nz, er_rows, width), BF16),
            pltpu.VMEM((nz, er_rows, width), BF16),
            pltpu.VMEM((nz, er_rows, width), BF16),
            pltpu.VMEM((2, nz, er_rows, width), BF16),
            pltpu.VMEM((4, 2, sr, er_rows), BF16),
            pltpu.VMEM((4, 2, sr, er_rows), BF16),
            pltpu.VMEM((2, nz, 4, n_sys, rows, width), BF16),
            pltpu.VMEM((n_sys, nz, 4, 2, rows, width), BF16),
            dma((3 + 3 * nz,)),
            dma((3,)), dma((3,)), dma((3,)), dma((3,)),
            dma((nz,)), dma((nz,)), dma((nz,)), dma((nz,)),
            dma((nz, 3)), dma((nz, 3)), dma((nz,)), dma((nz,)),
            dma((nz,)), dma((nz,)), dma((2, nz, 3)), dma((2, nz, 3)),
        ],
        compiler_params=pltpu.CompilerParams(collective_id=0, has_side_effects=True),
    )(atom_counts, inputs, out_grad, experts.reshape(er_rows, width), kl)
    return in_grad, expert_grad.reshape(n_exp, rows, width)


def plain(inputs, out_grad, coeff_fixed, atom_counts, experts):
    both = ("dp", "fsdp")
    n_sys, n_slots, width = inputs.shape
    n_exp, rows, _ = experts.shape
    coeffs = lax.all_gather(coeff_fixed, both, axis=0, tiled=True).astype(F32) / 4096.0
    valid = lax.broadcasted_iota(jnp.int32, (n_sys, n_slots), 1) < atom_counts[:, None]
    masked = jnp.where(valid[:, :, None], out_grad, jnp.zeros_like(out_grad))
    merged = jnp.einsum("se,eij->sij", coeffs, experts.astype(F32), precision=HIGH).astype(BF16)
    merged = lax.all_to_all(merged, both, split_axis=0, concat_axis=1, tiled=True)
    per_system = jnp.einsum("smi,smj->sij", inputs, masked, preferred_element_type=F32)
    per_system = lax.all_to_all(per_system, both, split_axis=1, concat_axis=0, tiled=True)
    expert_grad = jnp.einsum("se,sij->eij", coeffs, per_system, precision=HIGH)
    in_grad = jnp.einsum("smj,sij->smi", masked, merged, preferred_element_type=F32).astype(BF16)
    return in_grad, expert_grad


def solution(mesh):
    n_dp, n_fsdp = mesh.shape["dp"], mesh.shape["fsdp"]

    def shards(inputs, out_grad, coeff_fixed, atom_counts, experts):
        if n_dp % 4 == 0 and n_fsdp == 2 and experts.shape[1] % 16 == 0 and inputs.shape[0] <= 4:
            return fused(inputs, out_grad, coeff_fixed, atom_counts, experts, n_dp // 4)
        return plain(inputs, out_grad, coeff_fixed, atom_counts, experts)

    placed = (
        P(("dp", "fsdp"), None, None),
        P(("dp", "fsdp"), None, None),
        P(("dp", "fsdp"), None),
        P(("dp", "fsdp")),
        P(None, ("dp", "fsdp"), None),
    )
    return jax.shard_map(
        shards,
        mesh=mesh,
        in_specs=placed,
        out_specs=(P(("dp", "fsdp"), None, None), P(None, ("dp", "fsdp"), None)),
        check_vma=False,
    )
```

```python
import functools

import jax
import jax.numpy as jnp
from jax import lax
from jax.experimental import pallas as pl
from jax.experimental.pallas import tpu as pltpu
from jax.sharding import PartitionSpec as P

HIGH = lax.Precision.HIGHEST
MESH = pl.DeviceIdType.MESH
BF16 = jnp.bfloat16
F32 = jnp.float32
NEAR_ORDER = (5, 7, 4, 1, 6, 3, 2)


def dot(a, b, ca, cb):
    return lax.dot_general(a, b, (((ca,), (cb,)), ((), ())), preferred_element_type=F32)


def kernel(nz, n_sys, n_exp, rows, width,
           counts_ref, co_ref, in_ref, og_ref, ex_ref,
           ig_ref, eg_ref,
           mk, kl, ka, kt, pb, g, eo, zs, zr, xg, mb, mr,
           loc, ka_s, ka_r, xz_s, xz_r, pb_s, pb_r, zs_s, zs_r, mb_s, mb_r):
    dp = lax.axis_index("dp")
    y = lax.axis_index("fsdp")
    z = dp // 4
    x = lax.rem(dp // 2, 2)
    c = lax.rem(dp, 2)
    me = x * 4 + c * 2 + y
    sr = n_sys * rows
    er_rows = n_exp * rows

    def flip(v, d):
        return lax.rem(v + d, 2)

    def near(j):
        xx, cc, yy = flip(x, j // 4), flip(c, j // 2 % 2), flip(y, j % 2)
        return xx * 4 + cc * 2 + yy, ((z * 2 + xx) * 2 + cc, yy)

    def along(k):
        return ((lax.rem(z + k, nz) * 2 + x) * 2 + c, y)

    def zto(k):
        return lax.rem(z + k, nz)

    def zfrom(k):
        return lax.rem(z + nz - k, nz)

    plane = NEAR_ORDER
    peers = [near(j)[1] for j in plane] + [along(k) for k in range(1, nz)]
    barrier = pltpu.get_barrier_semaphore()
    for peer in peers:
        pl.semaphore_signal(barrier, inc=1, device_id=peer, device_id_type=MESH)

    col = lax.broadcasted_iota(jnp.int32, (rows, er_rows), 1)
    row = lax.broadcasted_iota(jnp.int32, (rows, er_rows), 0)
    owner, diagonal = col // rows, col % rows == row
    for s in range(n_sys):
        spread = jnp.zeros((rows, er_rows), jnp.int32)
        for e in range(n_exp):
            spread = jnp.where(owner == e, co_ref[s, e], spread)
        spread = jnp.where(diagonal, spread, 0)
        high = (spread // 64).astype(F32) / 64.0
        low = (spread % 64).astype(F32) / 4096.0
        kl[0, s * rows:(s + 1) * rows, :] = high.astype(BF16)
        kl[1, s * rows:(s + 1) * rows, :] = low.astype(BF16)
    pl.semaphore_wait(barrier, len(peers))

    def send(src, dst, s, r, peer):
        copy = pltpu.make_async_remote_copy(
            src_ref=src, dst_ref=dst, send_sem=s, recv_sem=r, device_id=peer, device_id_type=MESH
        )
        copy.start()
        return copy

    n_loc = [0]

    def local(src, dst):
        copy = pltpu.make_async_copy(src, dst, loc.at[n_loc[0]])
        n_loc[0] += 1
        copy.start()
        return copy

    sent = []
    xz_c = {}
    for k in range(1, nz):
        xz_c[k] = send(ex_ref, xg.at[k], xz_s.at[k], xz_r.at[k], along(k))
    ka_c = [send(kl, ka.at[me], ka_s.at[j - 1], ka_r.at[j - 1], near(j)[1]) for j in plane]
    ka_own = local(kl, ka.at[me])
    sent += ka_c + list(xz_c.values())

    for s in range(n_sys):
        slot = lax.broadcasted_iota(jnp.int32, og_ref.shape[1:], 0)
        mk[s] = jnp.where(slot < counts_ref[s], og_ref[s], jnp.zeros(og_ref.shape[1:], BF16))
        prod = dot(in_ref[s], mk[s], 0, 0).astype(BF16)
        for b in range(width // rows):
            pb[b % 8, b // 8, s * rows:(s + 1) * rows, :] = prod[b * rows:(b + 1) * rows, :]
    order = list(range(1, nz)) + [0]
    pb_c, g_own = {}, {}
    for k in order:
        for j in plane:
            to, peer = near(j)
            pb_c[k, j] = send(pb.at[to, zto(k)], g.at[k, me], pb_s.at[k, j - 1], pb_r.at[k, j - 1], peer)
        g_own[k] = local(pb.at[me, zto(k)], g.at[k, me])
    sent += list(pb_c.values())

    mb_c, m_own = {}, {}

    def merge(k, block):
        zz = zfrom(k)
        high = ka[:, 0].reshape(8 * sr, er_rows)
        low = ka[:, 1].reshape(8 * sr, er_rows)
        mb[k] = (dot(high, block, 1, 0) + dot(low, block, 1, 0)).astype(BF16).reshape(
            8, n_sys, rows, width)
        for j in plane:
            to, peer = near(j)
            mb_c[k, j] = send(mb.at[k, to], mr.at[:, zz, me], mb_s.at[k, j - 1], mb_r.at[k, j - 1], peer)
            sent.append(mb_c[k, j])
        m_own[k] = local(mb.at[k, me], mr.at[:, zz, me])

    zs_c = {}

    def reduce(k):
        g_own[k].wait()
        for j in plane:
            pb_c[k, j].wait_recv()
        block = g[k].reshape(8 * sr, width)
        total = dot(kt[0], block, 1, 0) + dot(kt[1], block, 1, 0)
        if k:
            zs[k] = total.astype(BF16)
            zs_c[k] = send(zs.at[k], zr.at[k], zs_s.at[k], zs_r.at[k], along(k))
            sent.append(zs_c[k])
        else:
            eo[...] = total

    def finish(k):
        m_own[k].wait()
        for j in plane:
            mb_c[k, j].wait_recv()
        zz = zfrom(k)
        span = 8 * rows
        lanes = pl.ds(pl.multiple_of(zz * span, span), span)
        for s in range(n_sys):
            ig_ref[s, :, lanes] = dot(mk[s], mr[s, zz].reshape(span, width), 1, 1).astype(BF16)

    ka_own.wait()
    for copy in ka_c:
        copy.wait_recv()
    merge(0, ex_ref[...])
    kt[0] = ka[:, 0].reshape(8 * sr, er_rows).T
    kt[1] = ka[:, 1].reshape(8 * sr, er_rows).T
    for k in range(1, nz):
        reduce(k)
        xz_c[k].wait_recv()
        merge(k, xg[k])
    reduce(0)
    finish(0)
    for k in range(1, nz):
        zs_c[k].wait_recv()
        eo[...] += zr[k].astype(F32)
        if k < nz - 1:
            finish(k)
    eg_ref[...] = eo[...]
    finish(nz - 1)
    for copy in sent:
        copy.wait_send()


def fused(inputs, out_grad, coeff_fixed, atom_counts, experts, nz):
    n_sys, n_slots, width = inputs.shape
    n_exp, rows, _ = experts.shape
    sr, er_rows = n_sys * rows, n_exp * rows
    vmem = pl.BlockSpec(memory_space=pltpu.VMEM)
    smem = pl.BlockSpec(memory_space=pltpu.SMEM)
    dma = pltpu.SemaphoreType.DMA
    in_grad, expert_grad = pl.pallas_call(
        functools.partial(kernel, nz, n_sys, n_exp, rows, width),
        out_shape=(
            jax.ShapeDtypeStruct(inputs.shape, BF16),
            jax.ShapeDtypeStruct((er_rows, width), F32),
        ),
        in_specs=[smem, smem, vmem, vmem, vmem],
        out_specs=(vmem, vmem),
        scratch_shapes=[
            pltpu.VMEM(out_grad.shape, BF16),
            pltpu.VMEM((2, sr, er_rows), BF16),
            pltpu.VMEM((8, 2, sr, er_rows), BF16),
            pltpu.VMEM((2, er_rows, 8 * sr), BF16),
            pltpu.VMEM((8, nz, sr, width), BF16),
            pltpu.VMEM((nz, 8, sr, width), BF16),
            pltpu.VMEM((er_rows, width), F32),
            pltpu.VMEM((nz, er_rows, width), BF16),
            pltpu.VMEM((nz, er_rows, width), BF16),
            pltpu.VMEM((nz, er_rows, width), BF16),
            pltpu.VMEM((nz, 8, n_sys, rows, width), BF16),
            pltpu.VMEM((n_sys, nz, 8, rows, width), BF16),
            dma((1 + 2 * nz,)),
            dma((7,)), dma((7,)), dma((nz,)), dma((nz,)),
            dma((nz, 7)), dma((nz, 7)), dma((nz,)), dma((nz,)),
            dma((nz, 7)), dma((nz, 7)),
        ],
        compiler_params=pltpu.CompilerParams(collective_id=0, has_side_effects=True),
    )(atom_counts, coeff_fixed, inputs, out_grad, experts.reshape(er_rows, width))
    return in_grad, expert_grad.reshape(n_exp, rows, width)


def plain(inputs, out_grad, coeff_fixed, atom_counts, experts):
    both = ("dp", "fsdp")
    n_sys, n_slots, width = inputs.shape
    n_exp, rows, _ = experts.shape
    coeffs = lax.all_gather(coeff_fixed, both, axis=0, tiled=True).astype(F32) / 4096.0
    valid = lax.broadcasted_iota(jnp.int32, (n_sys, n_slots), 1) < atom_counts[:, None]
    masked = jnp.where(valid[:, :, None], out_grad, jnp.zeros_like(out_grad))
    merged = jnp.einsum("se,eij->sij", coeffs, experts.astype(F32), precision=HIGH).astype(BF16)
    merged = lax.all_to_all(merged, both, split_axis=0, concat_axis=1, tiled=True)
    per_system = jnp.einsum("smi,smj->sij", inputs, masked, preferred_element_type=F32)
    per_system = lax.all_to_all(per_system, both, split_axis=1, concat_axis=0, tiled=True)
    expert_grad = jnp.einsum("se,sij->eij", coeffs, per_system, precision=HIGH)
    in_grad = jnp.einsum("smj,sij->smi", masked, merged, preferred_element_type=F32).astype(BF16)
    return in_grad, expert_grad


def solution(mesh):
    n_dp, n_fsdp = mesh.shape["dp"], mesh.shape["fsdp"]

    def shards(inputs, out_grad, coeff_fixed, atom_counts, experts):
        if n_dp % 4 == 0 and n_fsdp == 2 and experts.shape[1] % 16 == 0 and inputs.shape[0] <= 4 and inputs.shape[2] % 128 == 0:
            return fused(inputs, out_grad, coeff_fixed, atom_counts, experts, n_dp // 4)
        return plain(inputs, out_grad, coeff_fixed, atom_counts, experts)

    placed = (
        P(("dp", "fsdp"), None, None),
        P(("dp", "fsdp"), None, None),
        P(("dp", "fsdp"), None),
        P(("dp", "fsdp")),
        P(None, ("dp", "fsdp"), None),
    )
    return jax.shard_map(
        shards,
        mesh=mesh,
        in_specs=placed,
        out_specs=(P(("dp", "fsdp"), None, None), P(None, ("dp", "fsdp"), None)),
        check_vma=False,
    )
```

```python
import functools

import jax
import jax.numpy as jnp
from jax import lax
from jax.experimental import pallas as pl
from jax.experimental.pallas import tpu as pltpu
from jax.sharding import PartitionSpec as P

HIGH = lax.Precision.HIGHEST
MESH = pl.DeviceIdType.MESH
BF16 = jnp.bfloat16
F32 = jnp.float32
NEAR_ORDER = (5, 7, 4, 1, 6, 3, 2)


def dot(a, b, ca, cb):
    return lax.dot_general(a, b, (((ca,), (cb,)), ((), ())), preferred_element_type=F32)


def kernel(nz, n_sys, n_exp, rows, width,
           counts_ref, co_ref, in_ref, og_ref, ex_ref,
           ig_ref, eg_ref,
           mk, cl, ca, ka, kt, pb, g, eo, zs, zr, xg, mb, mr,
           loc, ka_s, ka_r, xz_s, xz_r, pb_s, pb_r, zs_s, zs_r, mb_s, mb_r):
    dp = lax.axis_index("dp")
    y = lax.axis_index("fsdp")
    z = dp // 4
    x = lax.rem(dp // 2, 2)
    c = lax.rem(dp, 2)
    me = x * 4 + c * 2 + y
    sr = n_sys * rows
    er_rows = n_exp * rows

    def flip(v, d):
        return lax.rem(v + d, 2)

    def near(j):
        xx, cc, yy = flip(x, j // 4), flip(c, j // 2 % 2), flip(y, j % 2)
        return xx * 4 + cc * 2 + yy, ((z * 2 + xx) * 2 + cc, yy)

    half = z // 2
    zm = z + half * (3 - 2 * z)

    def actual(v):
        return v + half * (3 - 2 * v)

    def line(v):
        return (actual(v) * 2 + x) * 2 + c, y

    def arrival(n):
        return actual((zm, 1 - zm, 2, 3)[n])

    def target(n):
        return actual((3, 2, 1 - zm, zm)[n])

    plane = NEAR_ORDER
    peers = [near(j)[1] for j in plane] + [((lax.rem(z + k, nz) * 2 + x) * 2 + c, y) for k in range(1, nz)]
    barrier = pltpu.get_barrier_semaphore()
    for peer in peers:
        pl.semaphore_signal(barrier, inc=1, device_id=peer, device_id_type=MESH)

    col = lax.broadcasted_iota(jnp.int32, cl.shape[1:], 1)
    row = lax.broadcasted_iota(jnp.int32, cl.shape[1:], 0)
    fixed = jnp.zeros(cl.shape[1:], jnp.int32)
    for s in range(n_sys):
        for e in range(n_exp):
            fixed = jnp.where((row == s) & (col == e), co_ref[s, e], fixed)
    cl[0] = ((fixed >> 6).astype(F32) / 64.0).astype(BF16)
    cl[1] = ((fixed & 63).astype(F32) / 4096.0).astype(BF16)
    pl.semaphore_wait(barrier, len(peers))

    def send(src, dst, s, r, peer):
        copy = pltpu.make_async_remote_copy(
            src_ref=src, dst_ref=dst, send_sem=s, recv_sem=r, device_id=peer, device_id_type=MESH
        )
        copy.start()
        return copy

    n_loc = [0]

    def local(src, dst):
        copy = pltpu.make_async_copy(src, dst, loc.at[n_loc[0]])
        n_loc[0] += 1
        copy.start()
        return copy

    sent = []
    ca_c = [send(cl, ca.at[me], ka_s.at[j - 1], ka_r.at[j - 1], near(j)[1]) for j in plane]
    ca_own = local(cl, ca.at[me])

    def relay(src, block, n, to):
        return pltpu.make_async_remote_copy(
            src_ref=src, dst_ref=xg.at[block], send_sem=xz_s.at[n], recv_sem=xz_r.at[block],
            device_id=to, device_id_type=MESH)

    relay(ex_ref, z, 0, line(1 - zm)).start()

    @pl.when(zm == 1)
    def _():
        relay(ex_ref, z, nz, line(2)).start()

    sent += ca_c

    for s in range(n_sys):
        slot = lax.broadcasted_iota(jnp.int32, og_ref.shape[1:], 0)
        mk[s] = jnp.where(slot < counts_ref[s], og_ref[s], jnp.zeros(og_ref.shape[1:], BF16))
        prod = dot(in_ref[s], mk[s], 0, 0).astype(BF16)
        for b in range(width // rows):
            pb[b % 8, b // 8, s * rows:(s + 1) * rows, :] = prod[b * rows:(b + 1) * rows, :]
    order = list(range(nz))
    pb_c, g_own = {}, {}
    for k in order:
        for j in plane:
            to, peer = near(j)
            pb_c[k, j] = send(pb.at[to, target(k)], g.at[k, me], pb_s.at[k, j - 1], pb_r.at[k, j - 1], peer)
        g_own[k] = local(pb.at[me, target(k)], g.at[k, me])
    sent += list(pb_c.values())

    mb_c, m_own = {}, {}

    def merge(k, block):
        zz = arrival(k)
        mb[k] = (dot(ka[0], block, 1, 0) + dot(ka[1], block, 1, 0)).astype(BF16).reshape(
            8, n_sys, rows, width)
        for j in plane:
            to, peer = near(j)
            mb_c[k, j] = send(mb.at[k, to], mr.at[:, zz, me], mb_s.at[k, j - 1], mb_r.at[k, j - 1], peer)
            sent.append(mb_c[k, j])
        m_own[k] = local(mb.at[k, me], mr.at[:, zz, me])

    zs_c = {}

    def landed(slot):
        pltpu.make_async_remote_copy(
            src_ref=zs.at[0], dst_ref=zr.at[slot], send_sem=zs_s.at[0], recv_sem=zs_r.at[slot],
            device_id=line(1 - zm), device_id_type=MESH).wait_recv()
        return zr[slot].astype(F32)

    def reduce(k):
        g_own[k].wait()
        for j in plane:
            pb_c[k, j].wait_recv()
        block = g[k].reshape(8 * sr, width)
        eo[k] = dot(kt[0], block, 1, 0) + dot(kt[1], block, 1, 0)

    def forward(k):
        @pl.when(zm == 1)
        def _():
            eo[k] += landed(k)

        zs[k] = eo[k].astype(BF16)
        slot = (2 * zm, 1 + 3 * zm, 3)[k]
        zs_c[k] = send(zs.at[k], zr.at[slot], zs_s.at[k], zs_r.at[slot],
                       line((zm + 1, zm + 1, 1 - zm)[k]))
        sent.append(zs_c[k])

    def finish(k):
        m_own[k].wait()
        for j in plane:
            mb_c[k, j].wait_recv()
        zz = arrival(k)
        span = 8 * rows
        lanes = pl.ds(pl.multiple_of(zz * span, span), span)
        for s in range(n_sys):
            ig_ref[s, :, lanes] = dot(mk[s], mr[s, zz].reshape(span, width), 1, 1).astype(BF16)

    ca_own.wait()
    for copy in ca_c:
        copy.wait_recv()
    lane = lax.broadcasted_iota(jnp.int32, (cl.shape[2], er_rows), 1)
    first = lax.broadcasted_iota(jnp.int32, (cl.shape[2], er_rows), 0) * rows
    pick = jnp.where((lane >= first) & (lane < first + rows), 1.0, 0.0).astype(BF16)
    wide = dot(ca[...].reshape(16 * cl.shape[1], cl.shape[2]), pick, 1, 0)
    across = lax.broadcasted_iota(jnp.int32, (rows, er_rows), 1) % rows
    diagonal = across == lax.broadcasted_iota(jnp.int32, (rows, er_rows), 0)
    for p in range(8):
        for h in range(2):
            for s in range(n_sys):
                at = (p * 2 + h) * cl.shape[1] + s
                value = jnp.broadcast_to(wide[at:at + 1, :], (rows, er_rows))
                spot = (p * n_sys + s) * rows
                ka[h, spot:spot + rows, :] = jnp.where(diagonal, value, 0.0).astype(BF16)
    merge(0, ex_ref[...])
    kt[0] = ka[0].T
    kt[1] = ka[1].T

    def arrived(n):
        block = arrival(n)
        copy = relay(ex_ref, block, n, line(1 - zm))
        copy.wait_recv()

        @pl.when(zm == 1)
        def _():
            relay(xg.at[block], block, n, line(2 if n == 1 else 0)).start()

        merge(n, xg[block])

    arrived(1)
    reduce(0)
    forward(0)
    arrived(2)
    reduce(1)
    forward(1)
    arrived(3)
    reduce(2)
    forward(2)
    reduce(3)
    finish(0)
    finish(1)
    finish(2)
    eg_ref[...] = eo[3] + landed(3)

    @pl.when(zm == 1)
    def _():
        eg_ref[...] += landed(4)

    finish(3)
    relay(ex_ref, z, 0, line(1 - zm)).wait_send()

    @pl.when(zm == 1)
    def _():
        relay(ex_ref, z, nz, line(2)).wait_send()
        for n in range(1, nz):
            relay(ex_ref, z, n, line(0)).wait_send()

    for copy in sent:
        copy.wait_send()


def fused(inputs, out_grad, coeff_fixed, atom_counts, experts, nz):
    n_sys, n_slots, width = inputs.shape
    n_exp, rows, _ = experts.shape
    sr, er_rows = n_sys * rows, n_exp * rows
    vmem = pl.BlockSpec(memory_space=pltpu.VMEM)
    smem = pl.BlockSpec(memory_space=pltpu.SMEM)
    dma = pltpu.SemaphoreType.DMA
    in_grad, expert_grad = pl.pallas_call(
        functools.partial(kernel, nz, n_sys, n_exp, rows, width),
        out_shape=(
            jax.ShapeDtypeStruct(inputs.shape, BF16),
            jax.ShapeDtypeStruct((er_rows, width), F32),
        ),
        in_specs=[smem, smem, vmem, vmem, vmem],
        out_specs=(vmem, vmem),
        scratch_shapes=[
            pltpu.VMEM(out_grad.shape, BF16),
            pltpu.VMEM((2, 16, 128), BF16),
            pltpu.VMEM((8, 2, 16, 128), BF16),
            pltpu.VMEM((2, 8 * sr, er_rows), BF16),
            pltpu.VMEM((2, er_rows, 8 * sr), BF16),
            pltpu.VMEM((8, nz, sr, width), BF16),
            pltpu.VMEM((nz, 8, sr, width), BF16),
            pltpu.VMEM((nz, er_rows, width), F32),
            pltpu.VMEM((nz - 1, er_rows, width), BF16),
            pltpu.VMEM((nz + 1, er_rows, width), BF16),
            pltpu.VMEM((nz, er_rows, width), BF16),
            pltpu.VMEM((nz, 8, n_sys, rows, width), BF16),
            pltpu.VMEM((n_sys, nz, 8, rows, width), BF16),
            dma((1 + 2 * nz,)),
            dma((7,)), dma((7,)), dma((nz + 1,)), dma((nz,)),
            dma((nz, 7)), dma((nz, 7)), dma((nz - 1,)), dma((nz + 1,)),
            dma((nz, 7)), dma((nz, 7)),
        ],
        compiler_params=pltpu.CompilerParams(collective_id=0, has_side_effects=True),
    )(atom_counts, coeff_fixed, inputs, out_grad, experts.reshape(er_rows, width))
    return in_grad, expert_grad.reshape(n_exp, rows, width)


def plain(inputs, out_grad, coeff_fixed, atom_counts, experts):
    both = ("dp", "fsdp")
    n_sys, n_slots, width = inputs.shape
    n_exp, rows, _ = experts.shape
    coeffs = lax.all_gather(coeff_fixed, both, axis=0, tiled=True).astype(F32) / 4096.0
    valid = lax.broadcasted_iota(jnp.int32, (n_sys, n_slots), 1) < atom_counts[:, None]
    masked = jnp.where(valid[:, :, None], out_grad, jnp.zeros_like(out_grad))
    merged = jnp.einsum("se,eij->sij", coeffs, experts.astype(F32), precision=HIGH).astype(BF16)
    merged = lax.all_to_all(merged, both, split_axis=0, concat_axis=1, tiled=True)
    per_system = jnp.einsum("smi,smj->sij", inputs, masked, preferred_element_type=F32)
    per_system = lax.all_to_all(per_system, both, split_axis=1, concat_axis=0, tiled=True)
    expert_grad = jnp.einsum("se,sij->eij", coeffs, per_system, precision=HIGH)
    in_grad = jnp.einsum("smj,sij->smi", masked, merged, preferred_element_type=F32).astype(BF16)
    return in_grad, expert_grad


def solution(mesh):
    n_dp, n_fsdp = mesh.shape["dp"], mesh.shape["fsdp"]

    def shards(inputs, out_grad, coeff_fixed, atom_counts, experts):
        n_sys, _, width = inputs.shape
        n_exp, rows, _ = experts.shape
        if n_dp == 16 and n_fsdp == 2 and rows % 16 == 0 and n_sys <= 16 and n_exp <= 128:
            return fused(inputs, out_grad, coeff_fixed, atom_counts, experts, n_dp // 4)
        return plain(inputs, out_grad, coeff_fixed, atom_counts, experts)

    placed = (
        P(("dp", "fsdp"), None, None),
        P(("dp", "fsdp"), None, None),
        P(("dp", "fsdp"), None),
        P(("dp", "fsdp")),
        P(None, ("dp", "fsdp"), None),
    )
    return jax.shard_map(
        shards,
        mesh=mesh,
        in_specs=placed,
        out_specs=(P(("dp", "fsdp"), None, None), P(None, ("dp", "fsdp"), None)),
        check_vma=False,
    )
```

```python
import functools

import jax
import jax.numpy as jnp
from jax import lax
from jax.experimental import pallas as pl
from jax.experimental.pallas import tpu as pltpu
from jax.sharding import PartitionSpec as P

HIGH = lax.Precision.HIGHEST
MESH = pl.DeviceIdType.MESH
BF16 = jnp.bfloat16
F32 = jnp.float32
NEAR_ORDER = (5, 7, 4, 1, 6, 3, 2)


def dot(a, b, ca, cb):
    return lax.dot_general(a, b, (((ca,), (cb,)), ((), ())), preferred_element_type=F32)


def kernel(nz, n_sys, n_exp, rows, width,
           counts_ref, co_ref, in_ref, og_ref, ex_ref,
           ig_ref, eg_ref,
           mk, cl, ca, ka, kt, pb, g, eo, zs, zr, xg, mb, mr,
           loc, ka_s, ka_r, xz_s, xz_r, pb_s, pb_r, zs_s, zs_r, mb_s, mb_r):
    dp = lax.axis_index("dp")
    y = lax.axis_index("fsdp")
    z = dp // 4
    x = lax.rem(dp // 2, 2)
    c = lax.rem(dp, 2)
    me = x * 4 + c * 2 + y
    sr = n_sys * rows
    er_rows = n_exp * rows

    def flip(v, d):
        return lax.rem(v + d, 2)

    def near(j):
        xx, cc, yy = flip(x, j // 4), flip(c, j // 2 % 2), flip(y, j % 2)
        return xx * 4 + cc * 2 + yy, ((z * 2 + xx) * 2 + cc, yy)

    half = z // 2
    zm = z + half * (3 - 2 * z)

    def actual(v):
        return v + half * (3 - 2 * v)

    def line(v):
        return (actual(v) * 2 + x) * 2 + c, y

    def arrival(n):
        return actual((zm, 1 - zm, 2, 3)[n])

    def target(n):
        return actual((3, 2, 1 - zm, zm)[n])

    plane = NEAR_ORDER
    peers = [near(j)[1] for j in plane] + [((lax.rem(z + k, nz) * 2 + x) * 2 + c, y) for k in range(1, nz)]
    barrier = pltpu.get_barrier_semaphore()
    for peer in peers:
        pl.semaphore_signal(barrier, inc=1, device_id=peer, device_id_type=MESH)

    col = lax.broadcasted_iota(jnp.int32, cl.shape[1:], 1)
    row = lax.broadcasted_iota(jnp.int32, cl.shape[1:], 0)
    fixed = jnp.zeros(cl.shape[1:], jnp.int32)
    for s in range(n_sys):
        for e in range(n_exp):
            fixed = jnp.where((row == s) & (col == e), co_ref[s, e], fixed)
    cl[0] = ((fixed >> 6).astype(F32) / 64.0).astype(BF16)
    cl[1] = ((fixed & 63).astype(F32) / 4096.0).astype(BF16)
    pl.semaphore_wait(barrier, len(peers))

    def send(src, dst, s, r, peer):
        copy = pltpu.make_async_remote_copy(
            src_ref=src, dst_ref=dst, send_sem=s, recv_sem=r, device_id=peer, device_id_type=MESH
        )
        copy.start()
        return copy

    n_loc = [0]

    def local(src, dst):
        copy = pltpu.make_async_copy(src, dst, loc.at[n_loc[0]])
        n_loc[0] += 1
        copy.start()
        return copy

    sent = []
    ca_c = [send(cl, ca.at[me], ka_s.at[j - 1], ka_r.at[j - 1], near(j)[1]) for j in plane]
    ca_own = local(cl, ca.at[me])

    def relay(src, block, n, to):
        return pltpu.make_async_remote_copy(
            src_ref=src, dst_ref=xg.at[block], send_sem=xz_s.at[n], recv_sem=xz_r.at[block],
            device_id=to, device_id_type=MESH)

    relay(ex_ref, z, 0, line(1 - zm)).start()

    @pl.when(zm == 1)
    def _():
        relay(ex_ref, z, nz, line(2)).start()

    sent += ca_c

    for s in range(n_sys):
        slot = lax.broadcasted_iota(jnp.int32, og_ref.shape[1:], 0)
        mk[s] = jnp.where(slot < counts_ref[s], og_ref[s], jnp.zeros(og_ref.shape[1:], BF16))
    pb_c, g_own = {}, {}
    for k in range(nz):
        span = 8 * rows
        lanes = pl.ds(pl.multiple_of(target(k) * span, span), span)
        for s in range(n_sys):
            prod = dot(in_ref[s, :, lanes], mk[s], 0, 0).astype(BF16)
            for b in range(8):
                pb[b, k, s * rows:(s + 1) * rows, :] = prod[b * rows:(b + 1) * rows, :]
        for j in plane:
            to, peer = near(j)
            pb_c[k, j] = send(pb.at[to, k], g.at[k, me], pb_s.at[k, j - 1], pb_r.at[k, j - 1], peer)
        g_own[k] = local(pb.at[me, k], g.at[k, me])
    sent += list(pb_c.values())

    mb_c, m_own = {}, {}

    def merge(k, block):
        zz = arrival(k)
        mb[k] = (dot(ka[0], block, 1, 0) + dot(ka[1], block, 1, 0)).astype(BF16).reshape(
            8, n_sys, rows, width)
        for j in plane:
            to, peer = near(j)
            mb_c[k, j] = send(mb.at[k, to], mr.at[:, zz, me], mb_s.at[k, j - 1], mb_r.at[k, j - 1], peer)
            sent.append(mb_c[k, j])
        m_own[k] = local(mb.at[k, me], mr.at[:, zz, me])

    def landed(slot):
        pltpu.make_async_remote_copy(
            src_ref=zs.at[0], dst_ref=zr.at[slot], send_sem=zs_s.at[0], recv_sem=zs_r.at[slot],
            device_id=line(1 - zm), device_id_type=MESH).wait_recv()
        return zr[slot].astype(F32)

    def reduce(k):
        g_own[k].wait()
        for j in plane:
            pb_c[k, j].wait_recv()
        block = g[k].reshape(8 * sr, width)
        eo[k] = dot(kt[0], block, 1, 0) + dot(kt[1], block, 1, 0)

    def onward(k):
        slot = (2 * zm, 1 + 3 * zm, 3)[k]
        return pltpu.make_async_remote_copy(
            src_ref=zs.at[k], dst_ref=zr.at[slot], send_sem=zs_s.at[k], recv_sem=zs_r.at[slot],
            device_id=line((zm + 1, zm + 1, 1 - zm)[k]), device_id_type=MESH)

    def begin(k):
        @pl.when(zm == 0)
        def _():
            zs[k] = eo[k].astype(BF16)
            onward(k).start()

    def proceed(k):
        @pl.when(zm == 1)
        def _():
            zs[k] = (eo[k] + landed(k)).astype(BF16)
            onward(k).start()

    def finish(k):
        m_own[k].wait()
        for j in plane:
            mb_c[k, j].wait_recv()
        zz = arrival(k)
        span = 8 * rows
        lanes = pl.ds(pl.multiple_of(zz * span, span), span)
        for s in range(n_sys):
            ig_ref[s, :, lanes] = dot(mk[s], mr[s, zz].reshape(span, width), 1, 1).astype(BF16)

    ca_own.wait()
    for copy in ca_c:
        copy.wait_recv()
    lane = lax.broadcasted_iota(jnp.int32, (cl.shape[2], er_rows), 1)
    first = lax.broadcasted_iota(jnp.int32, (cl.shape[2], er_rows), 0) * rows
    pick = jnp.where((lane >= first) & (lane < first + rows), 1.0, 0.0).astype(BF16)
    wide = dot(ca[...].reshape(16 * cl.shape[1], cl.shape[2]), pick, 1, 0)
    across = lax.broadcasted_iota(jnp.int32, (rows, er_rows), 1) % rows
    diagonal = across == lax.broadcasted_iota(jnp.int32, (rows, er_rows), 0)
    for p in range(8):
        for h in range(2):
            for s in range(n_sys):
                at = (p * 2 + h) * cl.shape[1] + s
                value = jnp.broadcast_to(wide[at:at + 1, :], (rows, er_rows))
                spot = (p * n_sys + s) * rows
                ka[h, spot:spot + rows, :] = jnp.where(diagonal, value, 0.0).astype(BF16)
    merge(0, ex_ref[...])
    kt[0] = ka[0].T
    kt[1] = ka[1].T

    def arrived(n):
        block = arrival(n)
        copy = relay(ex_ref, block, n, line(1 - zm))
        copy.wait_recv()

        @pl.when(zm == 1)
        def _():
            relay(xg.at[block], block, n, line(2 if n == 1 else 0)).start()

    arrived(1)
    reduce(0)
    begin(0)
    arrived(2)
    merge(1, xg[arrival(1)])
    reduce(1)
    begin(1)
    merge(2, xg[arrival(2)])
    arrived(3)
    proceed(0)
    merge(3, xg[arrival(3)])
    proceed(1)
    reduce(2)
    begin(2)
    proceed(2)
    reduce(3)
    finish(0)
    finish(1)
    finish(2)
    eg_ref[...] = eo[3] + landed(3)

    @pl.when(zm == 1)
    def _():
        eg_ref[...] += landed(4)

    finish(3)
    relay(ex_ref, z, 0, line(1 - zm)).wait_send()
    for k in range(nz - 1):
        onward(k).wait_send()

    @pl.when(zm == 1)
    def _():
        relay(ex_ref, z, nz, line(2)).wait_send()
        for n in range(1, nz):
            relay(ex_ref, z, n, line(0)).wait_send()

    for copy in sent:
        copy.wait_send()


def fused(inputs, out_grad, coeff_fixed, atom_counts, experts, nz):
    n_sys, n_slots, width = inputs.shape
    n_exp, rows, _ = experts.shape
    sr, er_rows = n_sys * rows, n_exp * rows
    vmem = pl.BlockSpec(memory_space=pltpu.VMEM)
    smem = pl.BlockSpec(memory_space=pltpu.SMEM)
    dma = pltpu.SemaphoreType.DMA
    in_grad, expert_grad = pl.pallas_call(
        functools.partial(kernel, nz, n_sys, n_exp, rows, width),
        out_shape=(
            jax.ShapeDtypeStruct(inputs.shape, BF16),
            jax.ShapeDtypeStruct((er_rows, width), F32),
        ),
        in_specs=[smem, smem, vmem, vmem, vmem],
        out_specs=(vmem, vmem),
        scratch_shapes=[
            pltpu.VMEM(out_grad.shape, BF16),
            pltpu.VMEM((2, 16, 128), BF16),
            pltpu.VMEM((8, 2, 16, 128), BF16),
            pltpu.VMEM((2, 8 * sr, er_rows), BF16),
            pltpu.VMEM((2, er_rows, 8 * sr), BF16),
            pltpu.VMEM((8, nz, sr, width), BF16),
            pltpu.VMEM((nz, 8, sr, width), BF16),
            pltpu.VMEM((nz, er_rows, width), F32),
            pltpu.VMEM((nz - 1, er_rows, width), BF16),
            pltpu.VMEM((nz + 1, er_rows, width), BF16),
            pltpu.VMEM((nz, er_rows, width), BF16),
            pltpu.VMEM((nz, 8, n_sys, rows, width), BF16),
            pltpu.VMEM((n_sys, nz, 8, rows, width), BF16),
            dma((1 + 2 * nz,)),
            dma((7,)), dma((7,)), dma((nz + 1,)), dma((nz,)),
            dma((nz, 7)), dma((nz, 7)), dma((nz - 1,)), dma((nz + 1,)),
            dma((nz, 7)), dma((nz, 7)),
        ],
        compiler_params=pltpu.CompilerParams(collective_id=0, has_side_effects=True),
    )(atom_counts, coeff_fixed, inputs, out_grad, experts.reshape(er_rows, width))
    return in_grad, expert_grad.reshape(n_exp, rows, width)


def plain(inputs, out_grad, coeff_fixed, atom_counts, experts):
    both = ("dp", "fsdp")
    n_sys, n_slots, width = inputs.shape
    n_exp, rows, _ = experts.shape
    coeffs = lax.all_gather(coeff_fixed, both, axis=0, tiled=True).astype(F32) / 4096.0
    valid = lax.broadcasted_iota(jnp.int32, (n_sys, n_slots), 1) < atom_counts[:, None]
    masked = jnp.where(valid[:, :, None], out_grad, jnp.zeros_like(out_grad))
    merged = jnp.einsum("se,eij->sij", coeffs, experts.astype(F32), precision=HIGH).astype(BF16)
    merged = lax.all_to_all(merged, both, split_axis=0, concat_axis=1, tiled=True)
    per_system = jnp.einsum("smi,smj->sij", inputs, masked, preferred_element_type=F32)
    per_system = lax.all_to_all(per_system, both, split_axis=1, concat_axis=0, tiled=True)
    expert_grad = jnp.einsum("se,sij->eij", coeffs, per_system, precision=HIGH)
    in_grad = jnp.einsum("smj,sij->smi", masked, merged, preferred_element_type=F32).astype(BF16)
    return in_grad, expert_grad


def solution(mesh):
    n_dp, n_fsdp = mesh.shape["dp"], mesh.shape["fsdp"]

    def shards(inputs, out_grad, coeff_fixed, atom_counts, experts):
        n_sys, _, width = inputs.shape
        n_exp, rows, _ = experts.shape
        if n_dp == 16 and n_fsdp == 2 and rows % 16 == 0 and n_sys <= 16 and n_exp <= 128:
            return fused(inputs, out_grad, coeff_fixed, atom_counts, experts, n_dp // 4)
        return plain(inputs, out_grad, coeff_fixed, atom_counts, experts)

    placed = (
        P(("dp", "fsdp"), None, None),
        P(("dp", "fsdp"), None, None),
        P(("dp", "fsdp"), None),
        P(("dp", "fsdp")),
        P(None, ("dp", "fsdp"), None),
    )
    return jax.shard_map(
        shards,
        mesh=mesh,
        in_specs=placed,
        out_specs=(P(("dp", "fsdp"), None, None), P(None, ("dp", "fsdp"), None)),
        check_vma=False,
    )
```
